768 devices in a mesh: ctx: 32 (over x, y), tp: 8 (over z_lo, core), grp: 3 (over z_hi).
Axes of the slice: x: 4, y: 8, z: 12 (z_hi: 3, z_lo: 4; z = z_hi * 4 + z_lo), core: 2. Of those that a mesh axis runs over, the one named last changes fastest.
Arguments:
- outer_gate: bfloat16 [12288, 8192], P(('ctx', 'grp'), 'tp'), may hold values from -60 to 60
- inner_gate: bfloat16 [12288, 8192], P(('ctx', 'grp'), 'tp'), may hold values from -6 to 6
- signal: bfloat16 [12288, 8192], P(('ctx', 'grp'), 'tp'), may hold values from -6 to 6
- residues: float32 [16, 8192], P(None, 'tp'), may hold values from -4 to 4
- log_rates: float32 [16, 8192], P(None, 'tp'), as said below
- norm_gain: bfloat16 [8192], P('tp'), may hold values from 0.5 to 1.5
- cotangent: bfloat16 [12288, 8192], P(('ctx', 'grp'), 'tp'), may hold values from -6 to 6
Outputs:
- output: bfloat16 [12288, 8192], P(('ctx', 'grp'), 'tp')
- grad_outer: bfloat16 [12288, 8192], P(('ctx', 'grp'), 'tp')
- grad_inner: bfloat16 [12288, 8192], P(('ctx', 'grp'), 'tp')
- grad_signal: bfloat16 [12288, 8192], P(('ctx', 'grp'), 'tp')
- residue_grads: float32 [16, 8192], P(None, 'tp')
- rate_grads: float32 [16, 8192], P(None, 'tp')
The draws below stay inside these ranges and needn't reach their ends.
Inputs may be any that keep to these rules, and one draw needn't show every extreme that they name: `log_rates`: each entry is the natural logarithm of a rate between 0.1 / 12288 and 1 / 24.
All inputs are finite; a program needn't handle non-finite values.
Results may differ from the reference program's by a relative error of at most 0.0029.
Values sent between devices are 32-bit elements; how exact they have to be, the bound alone decides.
A program may use at most 64 MiB of HBM per device.

```python
import math
import jax
import jax.numpy as jnp
from jax import lax

D = 8192
MODES = 16
TOK_DEV = 128
TOKENS = 12288


def draw_outer_gate(key, part):
    key_base, key_cols, key_rows = jax.random.split(jax.random.fold_in(key, 11), 3)
    columns = jnp.arange(D, dtype=jnp.float32) / D
    jitter = jnp.exp(jax.random.uniform(key_cols, (D,), jnp.float32, -0.3, 0.3))
    rows = 10.0 ** (jax.random.uniform(key_rows, (TOKENS, 1), jnp.float32) - 0.5)
    base = jax.random.truncated_normal(key_base, -4.0, 4.0, (TOKENS, D), jnp.float32)
    colscale = 10.0 ** (columns - 0.5) * jitter
    return (base * colscale[None, :] * rows).astype(jnp.bfloat16)


def draw_log_rates(key, part):
    key_pick, key_spot = jax.random.split(jax.random.fold_in(key, 23), 2)
    spot = jax.random.uniform(key_spot, (MODES, D), jnp.float32)
    pick = jax.random.uniform(key_pick, (MODES, D), jnp.float32)
    fast = jnp.log(1.0 / 64.0) + spot * jnp.log(64.0 / 24.0)
    slow = jnp.log(0.25 / TOKENS) + spot * jnp.log(8.0)
    share = 0.5
    return jnp.where(pick < share, slow, fast)


def block_scale(key, dims, cuts, smallest, largest):
    factor_of = 1.0
    for axis_at, blocks in cuts:
        steps = jax.random.uniform(jax.random.fold_in(jax.random.fold_in(key, 6), axis_at), (blocks,), jnp.float32, smallest / len(cuts), largest / len(cuts))
        factor_of = factor_of * jnp.repeat(jnp.exp(steps), dims[axis_at] // blocks).reshape((-1,) + (1,) * (len(dims) - 1 - axis_at))
    return factor_of


def scatter_about(rng, shape, scale, reach, cuts=(), kind=jnp.bfloat16):
    level = block_scale(rng, shape, cuts, -0.22, 0.18) if cuts else 1.0
    entries = jax.random.normal(rng, shape, jnp.float32) * scale * level
    return jnp.minimum(jnp.maximum(entries, -reach), reach).astype(kind)


def setup_inputs(seed: int = 0) -> dict:
    splits = jax.random.split(jax.random.key(seed), 8)
    return {
        "outer_gate": draw_outer_gate(jax.random.fold_in(splits[7], 71), 0),
        "inner_gate": scatter_about(splits[1], (TOKENS, D), 1.0, 6.0, ((0, 96), (1, 8))),
        "signal": scatter_about(splits[2], (TOKENS, D), 1.0, 6.0, ((0, 96), (1, 8))),
        "residues": scatter_about(splits[3], (MODES, D), 1.0, 4.0, ((1, 8),), jnp.float32),
        "log_rates": draw_log_rates(jax.random.fold_in(splits[7], 71), 0),
        "norm_gain": jnp.clip(1.0 + 0.1 * jax.random.normal(splits[5], (D,), jnp.float32), 0.5, 1.5).astype(jnp.bfloat16),
        "cotangent": scatter_about(splits[6], (TOKENS, D), 1.0, 6.0, ((0, 96), (1, 8))),
    }


def reference(outer_gate, inner_gate, signal, residues, log_rates, norm_gain, cotangent):
    block = min(16, TOK_DEV)
    gain_wide = norm_gain.astype(jnp.float32)

    def forward(outer, inner, values_in, residue_in, logs_in):
        product = (inner.astype(jnp.float32) * values_in.astype(jnp.float32)).reshape(-1, block, D)
        rates = jnp.exp(logs_in)
        lags = jnp.arange(block, dtype=jnp.float32)
        powers = jnp.exp(-rates[:, None, :] * lags[None, :, None])
        weights = residue_in * jnp.sqrt(2.0 * rates)
        taps = lax.optimization_barrier(jnp.sum(weights[:, None, :] * powers, axis=0))
        offsets = jnp.arange(block, dtype=jnp.int32)[:, None] - jnp.arange(block, dtype=jnp.int32)[None, :]
        toeplitz = jnp.where((offsets >= 0)[:, :, None], taps[jnp.maximum(offsets, 0)], 0.0)
        local_part = jnp.einsum('ijc,bjc->bic', toeplitz, product, precision=lax.Precision.HIGHEST)
        tails = powers[:, ::-1, :]
        partial_sums = jnp.einsum('bjc,mjc->bmc', product, tails, precision=lax.Precision.HIGHEST)
        stride = jnp.exp(-rates * block)

        def advance(state, piece):
            return (stride * state + piece, state)
        _, starts = lax.scan(advance, jnp.zeros((MODES, D), jnp.float32), partial_sums)
        heads = powers * jnp.exp(-rates)[:, None, :]
        carried = jnp.einsum('bmc,mic->bic', starts * weights[None], heads, precision=lax.Precision.HIGHEST)
        mixed = outer.astype(jnp.float32) * (local_part + carried).reshape(TOKENS, D)
        scale = lax.rsqrt(lax.optimization_barrier(jnp.sum(mixed * mixed, axis=1)) / D + 1e-06)
        return mixed * scale[:, None] * gain_wide[None, :]
    result, backward = jax.vjp(forward, outer_gate, inner_gate, signal, residues, log_rates)
    grads = backward(cotangent.astype(jnp.float32))
    factor = 1.0 / math.sqrt(TOKENS)
    return (result.astype(jnp.bfloat16), grads[0], grads[1], grads[2], grads[3] * factor, grads[4] * factor)
```

```python
import math

import jax
import jax.numpy as jnp
from jax import lax
from jax.experimental import pallas as pl
from jax.experimental.pallas import tpu as pltpu
from jax.sharding import PartitionSpec as P

D = 8192
MODES = 16
ROWS = 8
LANES = 128
NX, NY = 4, 8
MESH = pl.DeviceIdType.MESH
F32 = jnp.float32
BF16 = jnp.bfloat16


def kernel(
    nz, nt, length, factor,
    outer_hbm, inner_hbm, signal_hbm, cot_hbm, residues_ref, log_rates_ref, gain_ref,
    output_ref, gouter_ref, ginner_ref, gsignal_ref, rgrad_ref, agrad_ref,
    outer_v, inner_v, signal_v, cot_v,
    tokens_p, tokens_r, tokens_w, mixed_n, sums_a, sums_b, cols_a, cols_b,
    rho_s, root_s, lam_s, wts_s, big_s,
    box_z, box_zd, box_zg,
    tot_s, totd_s, totg_s, pre_z, pre_zd, pre_zg,
    box_y, box_yd, box_yg, box_x, box_xd, box_xg, ret_s, retd_s, retg_s, box_r, box_rd, box_rg,
    xin_s, state_in, stated_in, adj_in,
    prm_s, prm_y, prm_x, prm_z, prm_g, box_t,
    in_sem, send_sem, recv_sem,
):
    ctx = lax.axis_index("ctx")
    x, y = ctx // NY, lax.rem(ctx, NY)
    z = lax.axis_index("grp")
    t = lax.axis_index("tp")
    block = float(length)

    def rows(start, size):
        return pl.ds(pl.multiple_of(start, size), size)

    places = {
        "z": (nz, z, lambda q: {"grp": q}),
        "y": (NY, y, lambda q: {"ctx": x * NY + q}),
        "x": (NX, x, lambda q: {"ctx": q * NY + y}),
        "t": (nt, t, lambda q: {"tp": q}),
    }
    used = [0]

    class Exchange:
        def __init__(self, axis, box, size, piece=None):
            self.n, self.me, self.device = places[axis]
            self.box, self.size = box, size
            self.piece = piece or (lambda q: self.slot(self.me))
            self.first = used[0]
            used[0] += self.n - 1

        def slot(self, q):
            return self.box.at[rows(q * self.size, self.size)]

        def copy(self, k, landing):
            peer = lax.rem(self.me + k, self.n)
            source = lax.rem(self.me + self.n - k, self.n)
            return pltpu.make_async_remote_copy(
                src_ref=self.piece(peer),
                dst_ref=self.slot(source if landing else self.me),
                send_sem=send_sem.at[self.first + k - 1],
                recv_sem=recv_sem.at[self.first + k - 1],
                device_id=self.device(peer),
                device_id_type=MESH,
            )

        def start(self):
            for k in range(1, self.n):
                self.copy(k, False).start()

        def wait(self):
            for k in range(1, self.n):
                self.copy(k, True).wait_recv()

        def drain(self):
            for k in range(1, self.n):
                self.copy(k, False).wait_send()

    span = MODES * ROWS
    own = 2 * ROWS
    mine = rows(y * own, own)

    def pick(ref):
        return lambda q: ref.at[rows(q * own, own)]

    gather_z = Exchange("z", box_z, span)
    gather_zd = Exchange("z", box_zd, span)
    gather_zg = Exchange("z", box_zg, span)
    split_y = Exchange("y", box_y, own, pick(tot_s))
    split_yd = Exchange("y", box_yd, own, pick(totd_s))
    split_yg = Exchange("y", box_yg, own, pick(totg_s))
    gather_x = Exchange("x", box_x, own)
    gather_xd = Exchange("x", box_xd, own)
    gather_xg = Exchange("x", box_xg, own)
    back_y = Exchange("y", box_r, own, pick(ret_s))
    back_yd = Exchange("y", box_rd, own, pick(retd_s))
    back_yg = Exchange("y", box_rg, own, pick(retg_s))
    norms = Exchange("t", box_t, ROWS)
    prm_split = Exchange("y", prm_y, 2 * own, lambda q: prm_s.at[rows(q * 2 * own, 2 * own)])
    prm_sum_x = Exchange("x", prm_x, 2 * own)
    prm_sum_z = Exchange("z", prm_z, 2 * own)
    prm_back = Exchange("y", prm_g, 2 * own)
    everything = [
        gather_z, gather_zd, gather_zg, split_y, split_yd, split_yg, gather_x, gather_xd, gather_xg,
        back_y, back_yd, back_yg, norms, prm_split, prm_sum_x, prm_sum_z, prm_back,
    ]

    loads = [
        pltpu.make_async_copy(src, dst, in_sem.at[i])
        for i, (src, dst) in enumerate(
            [(inner_hbm, inner_v), (signal_hbm, signal_v), (outer_hbm, outer_v), (cot_hbm, cot_v)]
        )
    ]
    for load in loads:
        load.start()

    barrier = pltpu.get_barrier_semaphore()
    partners = 0
    for axis in ("z", "y", "x", "t"):
        n, me, device = places[axis]
        for k in range(1, n):
            pl.semaphore_signal(
                barrier, inc=1, device_id=device(lax.rem(me + k, n)), device_id_type=MESH
            )
            partners += 1

    for half in range(MODES // 8):
        for j in range(ROWS):
            there = pl.ds(half * 64 + j, 8, stride=ROWS)
            lanes = slice(j * LANES, (j + 1) * LANES)
            rho = jnp.exp(log_rates_ref[half * 8 : half * 8 + 8, lanes])
            root = jnp.sqrt(2.0 * rho)
            rho_s[there, :] = rho
            root_s[there, :] = root
            wts_s[there, :] = residues_ref[half * 8 : half * 8 + 8, lanes] * root
    lam_s[...] = jnp.exp(-rho_s[...])
    big_s[...] = jnp.exp(-block * rho_s[...])

    def mode(ref, m, base=0):
        return ref[base + m * ROWS : base + (m + 1) * ROWS, :]

    def put(ref, m, value, base=0):
        ref[base + m * ROWS : base + (m + 1) * ROWS, :] = value

    def natural(body, step=16):
        def turn(i, carry):
            tokens = rows(i * step, step)
            for j in range(ROWS):
                body(tokens, j, slice(j * LANES, (j + 1) * LANES),
                     pl.ds(i * (step * ROWS) + j, step, stride=ROWS))
            return carry

        lax.fori_loop(0, length // step, turn, 0)

    def sweep(body, carry, unroll=8, reverse=False):
        def turn(i, carry):
            for u in range(unroll):
                at = i * unroll + u
                if reverse:
                    at = length - 1 - at
                carry = body(rows(at * ROWS, ROWS), carry)
            return carry

        return lax.fori_loop(0, length // unroll, turn, carry)

    zero = jnp.zeros((ROWS, LANES), F32)

    loads[0].wait()
    loads[1].wait()

    def multiply(tokens, j, lanes, place):
        tokens_p[place, :] = inner_v[tokens, lanes].astype(F32) * signal_v[tokens, lanes].astype(F32)

    natural(multiply)

    decay = [mode(lam_s, m) for m in range(MODES)]

    def leave(at, state):
        p = tokens_p[at, :]
        return tuple(d * s + p for d, s in zip(decay, state))

    state = sweep(leave, (zero,) * MODES)
    for m in range(MODES):
        box_z[rows(z * span + m * ROWS, ROWS), :] = state[m]

    pl.semaphore_wait(barrier, partners)
    gather_z.start()

    for half in range(2):
        some = range(half * 8, half * 8 + 8)
        decay = [mode(lam_s, m) for m in some]
        weight = [mode(wts_s, m) for m in some]

        def respond(at, carry, decay=decay, weight=weight, half=half):
            p = tokens_p[at, :]
            lagged = [d * (a + s) for d, a, s in zip(decay, carry[8:], carry[:8])]
            state = [d * s + p for d, s in zip(decay, carry[:8])]
            terms = [w * s for w, s in zip(weight, state)]
            while len(terms) > 1:
                terms = [a + b for a, b in zip(terms[::2], terms[1::2])]
            tokens_r[at, :] = terms[0] if half == 0 else tokens_r[at, :] + terms[0]
            return tuple(state + lagged)

        carry = sweep(respond, (zero,) * 16)
        for i, m in enumerate(some):
            box_zd[rows(z * span + m * ROWS, ROWS), :] = carry[8 + i]
    gather_zd.start()

    rho_own = rho_s[mine, :]
    step_y = jnp.exp((-nz * block) * rho_own)
    step_x = jnp.exp((-nz * NY * block) * rho_own)

    def total_z(box, total, pre, forward):
        order = range(nz) if forward else range(nz - 1, -1, -1)
        for m in range(MODES):
            hop = mode(big_s, m)
            running, chosen = zero, zero
            for q in order:
                chosen = jnp.where(z == q, running, chosen)
                running = hop * running + mode(box, m, q * span)
            put(total, m, running)
            put(pre, m, chosen)

    def prefix_y(box, pre, box_next, forward):
        order = range(NY) if forward else range(NY - 1, -1, -1)
        running = jnp.zeros((own, LANES), F32)
        for q in order:
            pre[q * own : (q + 1) * own, :] = running
            running = step_y * running + box[q * own : (q + 1) * own, :]
        box_next[rows(x * own, own), :] = running

    def return_y(box, pre, forward):
        order = range(NX) if forward else range(NX - 1, -1, -1)
        came = jnp.zeros((own, LANES), F32)
        for q in order:
            earlier = (q < x) if forward else (q > x)
            came = jnp.where(earlier, step_x * came + box[q * own : (q + 1) * own, :], came)
        xin_s[...] = came
        for q in (range(NY) if forward else range(NY - 1, -1, -1)):
            pre[q * own : (q + 1) * own, :] = pre[q * own : (q + 1) * own, :] + came
            came = step_y * came

    def keep_own(box, source):
        box[mine, :] = source[mine, :]

    def power_z(m, count):
        hop = mode(big_s, m)
        power, chosen = jnp.ones_like(hop), jnp.ones_like(hop)
        for q in range(1, nz):
            power = power * hop
            chosen = jnp.where(count == q, power, chosen)
        return chosen

    gather_z.wait()
    total_z(box_z, tot_s, pre_z, True)
    split_y.start()
    keep_own(box_y, tot_s)
    split_y.wait()
    prefix_y(box_y, ret_s, box_x, True)
    gather_x.start()
    gather_x.wait()
    return_y(box_x, ret_s, True)
    back_y.start()
    keep_own(box_r, ret_s)

    gather_zd.wait()
    for m in range(MODES):
        hop = mode(big_s, m)
        run, rund, chosen = zero, zero, zero
        for q in range(nz):
            chosen = jnp.where(z == q, rund, chosen)
            rund = hop * (rund + block * run) + mode(box_zd, m, q * span)
            run = hop * run + mode(box_z, m, q * span)
        put(totd_s, m, rund)
        put(pre_zd, m, chosen)
    split_yd.start()
    keep_own(box_yd, totd_s)

    loads[2].wait()
    loads[3].wait()
    back_y.wait()
    for m in range(MODES):
        put(state_in, m, mode(pre_z, m) + power_z(m, z) * mode(box_r, m))

    decay = [mode(lam_s, m) for m in range(MODES)]
    fade = tuple(mode(wts_s, m) * mode(state_in, m) for m in range(MODES))

    def carried(at, fade):
        fade = tuple(d * f for d, f in zip(decay, fade))
        terms = list(fade)
        while len(terms) > 1:
            terms = [a + b for a, b in zip(terms[::2], terms[1::2])]
        tokens_r[at, :] = tokens_r[at, :] + terms[0]
        return fade

    sweep(carried, fade)

    def mix(i, carry):
        tokens = rows(i * 16, 16)
        squares = jnp.zeros((16, LANES), F32)
        inners = jnp.zeros((16, LANES), F32)
        for j in range(ROWS):
            lanes = slice(j * LANES, (j + 1) * LANES)
            mixed = outer_v[tokens, lanes].astype(F32) * tokens_r[pl.ds(i * 128 + j, 16, stride=ROWS), :]
            gained = cot_v[tokens, lanes].astype(F32) * gain_ref[:, lanes]
            mixed_n[tokens, lanes] = mixed
            squares = squares + mixed * mixed
            inners = inners + gained * mixed
        sums_a[tokens, :] = squares
        sums_b[tokens, :] = inners
        return carry

    lax.fori_loop(0, length // 16, mix, 0)

    def across(a, b):
        return lax.dot_general(
            a, b, (((1,), (1,)), ((), ())), precision=lax.Precision.HIGHEST,
            preferred_element_type=F32,
        )

    ones = jnp.ones((ROWS, LANES), F32)
    upper = lax.broadcasted_iota(jnp.int32, (ROWS, length), 0) < 4
    box_t[rows(t * ROWS, ROWS), :] = jnp.where(
        upper, across(ones, sums_a[...]), across(ones, sums_b[...])
    )
    norms.start()

    split_yd.wait()
    run = jnp.zeros((own, LANES), F32)
    rund = run
    for q in range(NY):
        retd_s[q * own : (q + 1) * own, :] = rund
        rund = step_y * (rund + (nz * block) * run) + box_yd[q * own : (q + 1) * own, :]
        run = step_y * run + box_y[q * own : (q + 1) * own, :]
    box_xd[rows(x * own, own), :] = rund
    gather_xd.start()

    norms.wait()
    both = jnp.zeros((ROWS, length), F32)
    for q in range(nt):
        both = both + box_t[q * ROWS : (q + 1) * ROWS, :]
    scale = lax.rsqrt(both[0:1, :] / D + 1e-06)
    pull = scale * scale * scale * both[4:5, :] / D
    row_id = lax.broadcasted_iota(jnp.int32, (length, length), 0)
    col_id = lax.broadcasted_iota(jnp.int32, (length, length), 1)
    square = jnp.ones((LANES, length), F32)
    cols_a[...] = across(jnp.where(row_id == col_id, scale, 0.0), square)
    cols_b[...] = across(jnp.where(row_id == col_id, pull, 0.0), square)

    def finish(i, carry):
        tokens = rows(i * 16, 16)
        a, b = cols_a[tokens, :], cols_b[tokens, :]
        for j in range(ROWS):
            lanes = slice(j * LANES, (j + 1) * LANES)
            place = pl.ds(i * 128 + j, 16, stride=ROWS)
            mixed = mixed_n[tokens, lanes]
            gain = gain_ref[:, lanes]
            gained = cot_v[tokens, lanes].astype(F32) * gain
            grad = a * gained - mixed * b
            tokens_w[place, :] = grad * outer_v[tokens, lanes].astype(F32)
            output_ref[tokens, lanes] = (mixed * a * gain).astype(BF16)
            gouter_ref[tokens, lanes] = (grad * tokens_r[place, :]).astype(BF16)
        return carry

    lax.fori_loop(0, length // 16, finish, 0)

    def leave_back(at, adjoint):
        w = tokens_w[at, :]
        return tuple(d * a + w for d, a in zip(decay, adjoint))

    adjoint = sweep(leave_back, (zero,) * MODES, reverse=True)
    for m in range(MODES):
        box_zg[rows(z * span + m * ROWS, ROWS), :] = decay[m] * adjoint[m]
    gather_zg.start()

    gather_xd.wait()
    came = jnp.zeros((own, LANES), F32)
    camed = came
    for q in range(NX):
        camed = jnp.where(
            q < x,
            step_x * (camed + (nz * NY * block) * came) + box_xd[q * own : (q + 1) * own, :],
            camed,
        )
        came = jnp.where(q < x, step_x * came + box_x[q * own : (q + 1) * own, :], came)
    for q in range(NY):
        retd_s[q * own : (q + 1) * own, :] = retd_s[q * own : (q + 1) * own, :] + camed
        camed = step_y * (camed + (nz * block) * came)
        came = step_y * came
    back_yd.start()
    keep_own(box_rd, retd_s)

    for half in range(2):
        some = range(half * 8, half * 8 + 8)
        decay8 = [mode(lam_s, m) for m in some]
        weight8 = [mode(wts_s, m) for m in some]

        def pull_back(at, adjoint, decay=decay8, weight=weight8, half=half):
            w = tokens_w[at, :]
            adjoint = tuple(d * a + w for d, a in zip(decay, adjoint))
            terms = [k * a for k, a in zip(weight, adjoint)]
            while len(terms) > 1:
                terms = [a + b for a, b in zip(terms[::2], terms[1::2])]
            mixed_rows[at, :] = terms[0] if half == 0 else mixed_rows[at, :] + terms[0]
            return adjoint

        mixed_rows = tokens_r
        sweep(pull_back, (zero,) * 8, reverse=True)

    back_yd.wait()
    zf = z.astype(F32)
    for m in range(MODES):
        start_d = mode(box_rd, m) + (block * zf) * mode(box_r, m)
        put(stated_in, m, mode(pre_zd, m) + power_z(m, z) * start_d)

    for half in range(2):
        some = range(half * 8, half * 8 + 8)
        decay8 = [mode(lam_s, m) for m in some]

        def correlate(at, carry, decay=decay8):
            p, w = tokens_p[at, :], tokens_w[at, :]
            state, lagged, first, second = carry[:8], carry[8:16], carry[16:24], carry[24:]
            lagged = [d * (a + s) for d, a, s in zip(decay, lagged, state)]
            state = [d * s + p for d, s in zip(decay, state)]
            first = [f + w * s for f, s in zip(first, state)]
            second = [f + w * a for f, a in zip(second, lagged)]
            return tuple(state + lagged + first + second)

        carry = sweep(
            correlate,
            tuple(mode(state_in, m) for m in some)
            + tuple(mode(stated_in, m) for m in some)
            + (zero,) * 16,
            unroll=4,
        )
        for i, m in enumerate(some):
            base = (m // 2) * 2 * own + (m % 2) * ROWS
            prm_s[base : base + ROWS, :] = carry[16 + i]
            prm_s[base + own : base + own + ROWS, :] = carry[24 + i]
    prm_split.start()
    prm_y[rows(y * 2 * own, 2 * own), :] = prm_s[rows(y * 2 * own, 2 * own), :]

    def add_up(box, n):
        total = box[0 : 2 * own, :]
        for q in range(1, n):
            total = total + box[q * 2 * own : (q + 1) * 2 * own, :]
        return total

    gather_zg.wait()
    total_z(box_zg, totg_s, pre_zg, False)
    split_yg.start()
    keep_own(box_yg, totg_s)
    prm_split.wait()
    prm_x[rows(x * 2 * own, 2 * own), :] = add_up(prm_y, NY)
    prm_sum_x.start()
    split_yg.wait()
    prefix_y(box_yg, retg_s, box_xg, False)
    gather_xg.start()
    prm_sum_x.wait()
    prm_z[rows(z * 2 * own, 2 * own), :] = add_up(prm_x, NX)
    prm_sum_z.start()
    gather_xg.wait()
    return_y(box_xg, retg_s, False)
    back_yg.start()
    keep_own(box_rg, retg_s)
    prm_sum_z.wait()
    prm_g[rows(y * 2 * own, 2 * own), :] = add_up(prm_z, nz)
    prm_back.start()

    back_yg.wait()
    for m in range(MODES):
        put(adj_in, m, mode(pre_zg, m) + power_z(m, nz - 1 - z) * mode(box_rg, m))
    fade = tuple(mode(wts_s, m) * mode(adj_in, m) for m in range(MODES))

    def carried_back(at, fade):
        terms = list(fade)
        while len(terms) > 1:
            terms = [a + b for a, b in zip(terms[::2], terms[1::2])]
        tokens_r[at, :] = tokens_r[at, :] + terms[0]
        return tuple(d * f for d, f in zip(decay, fade))

    sweep(carried_back, fade, reverse=True)

    def last(tokens, j, lanes, place):
        grad = tokens_r[place, :]
        ginner_ref[tokens, lanes] = (grad * signal_v[tokens, lanes].astype(F32)).astype(BF16)
        gsignal_ref[tokens, lanes] = (grad * inner_v[tokens, lanes].astype(F32)).astype(BF16)

    natural(last)

    prm_back.wait()
    prm_split.drain()
    for m in range(MODES):
        base = (m // 2) * 2 * own + (m % 2) * ROWS
        first = prm_g[base : base + ROWS, :]
        second = prm_g[base + own : base + own + ROWS, :]
        put(prm_s, m, factor * (mode(root_s, m) * first))
        put(prm_s, m, factor * (mode(wts_s, m) * (0.5 * first - mode(rho_s, m) * second)), span)
    for half in range(MODES // 8):
        for j in range(ROWS):
            lanes = slice(j * LANES, (j + 1) * LANES)
            rgrad_ref[half * 8 : half * 8 + 8, lanes] = prm_s[pl.ds(half * 64 + j, 8, stride=ROWS), :]
            agrad_ref[half * 8 : half * 8 + 8, lanes] = prm_s[
                pl.ds(span + half * 64 + j, 8, stride=ROWS), :
            ]
    for exchange in everything:
        if exchange is not prm_split:
            exchange.drain()


def solution(mesh):
    nz, nt = mesh.shape["grp"], mesh.shape["tp"]
    blocks = mesh.shape["ctx"] * nz
    assert mesh.shape["ctx"] == NX * NY

    def step(outer_gate, inner_gate, signal, residues, log_rates, norm_gain, cotangent):
        length, channels = outer_gate.shape
        assert channels == ROWS * LANES and length == LANES and residues.shape[0] == MODES
        factor = 1.0 / math.sqrt(length * blocks)
        span, own = MODES * ROWS, 2 * ROWS

        def f32(count):
            return pltpu.VMEM((count, LANES), F32)

        wide = pltpu.VMEM((length, channels), BF16)
        exchanges = 4 * (nz - 1) + 8 * (NY - 1) + 4 * (NX - 1) + (nt - 1)
        scratch = (
            [wide] * 4
            + [f32(length * ROWS)] * 3
            + [pltpu.VMEM((length, channels), F32)]
            + [f32(length)] * 4
            + [f32(span)] * 5
            + [f32(nz * span)] * 3
            + [f32(span)] * 6
            + [f32(NY * own)] * 3
            + [f32(NX * own)] * 3
            + [f32(NY * own)] * 6
            + [f32(own)]
            + [f32(span)] * 3
            + [f32(2 * span), f32(2 * NY * own), f32(2 * NX * own), f32(2 * nz * own), f32(2 * NY * own)]
            + [f32(nt * ROWS)]
            + [
                pltpu.SemaphoreType.DMA((4,)),
                pltpu.SemaphoreType.DMA((exchanges,)),
                pltpu.SemaphoreType.DMA((exchanges,)),
            ]
        )
        vmem = pl.BlockSpec(memory_space=pltpu.VMEM)
        hbm = pl.BlockSpec(memory_space=pl.ANY)
        tokens = jax.ShapeDtypeStruct((length, channels), BF16)
        params = jax.ShapeDtypeStruct(residues.shape, F32)

        def body(*refs):
            kernel(nz, nt, length, factor, *refs)

        return pl.pallas_call(
            body,
            out_shape=(tokens,) * 4 + (params,) * 2,
            in_specs=[hbm] * 4 + [vmem] * 3,
            out_specs=(vmem,) * 6,
            scratch_shapes=scratch,
            compiler_params=pltpu.CompilerParams(
                collective_id=0, has_side_effects=True, vmem_limit_bytes=40 * 1024 * 1024
            ),
            name="hyena",
        )(
            outer_gate, inner_gate, signal, cotangent, residues, log_rates,
            norm_gain.astype(F32)[None, :],
        )

    wide, narrow = P(("ctx", "grp"), "tp"), P(None, "tp")
    return jax.shard_map(
        step,
        mesh=mesh,
        in_specs=(wide, wide, wide, narrow, narrow, P("tp"), wide),
        out_specs=(wide,) * 4 + (narrow,) * 2,
        check_vma=False,
    )
```

```python
import math

import jax
import jax.numpy as jnp
from jax import lax
from jax.experimental import pallas as pl
from jax.experimental.pallas import tpu as pltpu
from jax.sharding import PartitionSpec as P

D = 8192
MODES = 16
ROWS = 8
LANES = 128
NX, NY = 4, 8
MESH = pl.DeviceIdType.MESH
F32 = jnp.float32
BF16 = jnp.bfloat16
HALF = MODES // 2
FLOWS = ("s_first", "s_last", "d_first", "d_last", "g_first", "g_last")


def layout(nz, nt, length):
    span, own = HALF * ROWS, ROWS
    shapes = {"tokens_p": length * ROWS, "tokens_r": length * ROWS, "tokens_w": length * ROWS}
    for name in ("sums_a", "sums_b", "cols_a", "cols_b"):
        shapes[name] = length
    for name in ("rho_s", "root_s", "lam_s", "wts_s", "big_s", "state_in", "stated_in", "adj_in"):
        shapes[name] = MODES * ROWS
    for flow in FLOWS:
        shapes |= {
            flow + ".loc": span, flow + ".out": nz * span, flow + ".box_z": nz * span,
            flow + ".tot": span, flow + ".pre": span, flow + ".box_y": NY * own,
            flow + ".box_x": NX * own, flow + ".ret": NY * own, flow + ".box_r": NY * own,
        }
    pair = 4 * ROWS
    shapes |= {
        "prm_s": NY * pair, "prm_y": NY * pair, "prm_x": NX * pair, "prm_z": nz * pair,
        "prm_g": NY * pair, "fin_s": 2 * MODES * ROWS, "box_t": nt * ROWS,
    }
    return shapes


def kernel(
    nz, nt, length, factor,
    outer_hbm, inner_hbm, signal_hbm, cot_hbm, residues_hbm, log_rates_hbm, gain_hbm,
    output_ref, gouter_ref, ginner_ref, gsignal_ref, rgrad_ref, agrad_ref,
    outer_v, inner_v, signal_v, cot_v, residues_v, log_rates_v, gain_v, gain_ref, mixed_n,
    in_sem, send_sem, recv_sem, *scratch,
):
    at = dict(zip(layout(nz, nt, length), scratch))
    tokens_p, tokens_r, tokens_w = at["tokens_p"], at["tokens_r"], at["tokens_w"]
    rho_s, root_s, lam_s, wts_s, big_s = (at[k] for k in ("rho_s", "root_s", "lam_s", "wts_s", "big_s"))
    prm_s, prm_y, prm_x, prm_z, prm_g = (at[k] for k in ("prm_s", "prm_y", "prm_x", "prm_z", "prm_g"))
    box_t, fin_s = at["box_t"], at["fin_s"]

    ctx = lax.axis_index("ctx")
    x, y = ctx // NY, lax.rem(ctx, NY)
    z = lax.axis_index("grp")
    t = lax.axis_index("tp")
    block = float(length)

    def rows(start, size):
        return pl.ds(pl.multiple_of(start, size), size)

    places = {
        "z": (nz, z, lambda q: {"grp": q}),
        "y": (NY, y, lambda q: {"ctx": x * NY + q}),
        "x": (NX, x, lambda q: {"ctx": q * NY + y}),
        "t": (nt, t, lambda q: {"tp": q}),
    }
    used = [0]
    everything = []

    class Exchange:
        def __init__(self, axis, box, size, piece=None):
            self.n, self.me, self.device = places[axis]
            self.box, self.size = box, size
            self.piece = piece or (lambda q: self.slot(self.me))
            self.first = used[0]
            used[0] += self.n - 1
            self.far_first = sorted(range(1, self.n), key=lambda k: -min(k, self.n - k))
            everything.append(self)

        def slot(self, q):
            return self.box.at[rows(q * self.size, self.size)]

        def copy(self, k, landing):
            peer = lax.rem(self.me + k, self.n)
            source = lax.rem(self.me + self.n - k, self.n)
            return pltpu.make_async_remote_copy(
                src_ref=self.piece(peer),
                dst_ref=self.slot(source if landing else self.me),
                send_sem=send_sem.at[self.first + k - 1],
                recv_sem=recv_sem.at[self.first + k - 1],
                device_id=self.device(peer),
                device_id_type=MESH,
            )

        def start(self):
            for k in self.far_first:
                self.copy(k, False).start()

        def wait(self):
            for k in range(1, self.n):
                self.copy(k, True).wait_recv()

        def drain(self):
            for k in range(1, self.n):
                self.copy(k, False).wait_send()

    span, own = HALF * ROWS, ROWS
    mine = rows(y * own, own)
    zero = jnp.zeros((ROWS, LANES), F32)

    def mode(ref, m, base=0):
        return ref[base + m * ROWS : base + (m + 1) * ROWS, :]

    def put(ref, m, value, base=0):
        ref[base + m * ROWS : base + (m + 1) * ROWS, :] = value

    def advance(value, low, power, count):
        return power * value if low is None else power * (value + (block * count) * low)

    class Flow:
        def __init__(self, name, first, forward, low=None):
            self.first, self.low = first, low
            self.m0 = 0 if first else HALF
            for key in ("loc", "out", "box_z", "tot", "pre", "box_y", "box_x", "ret", "box_r"):
                setattr(self, key, at[name + "." + key])
            self.zi = z if forward else nz - 1 - z
            self.order = lambda n: range(n) if forward else range(n - 1, -1, -1)
            self.place = lambda q: q if forward else nz - 1 - q
            self.before = (lambda q: q < x) if forward else (lambda q: q > x)
            self.ex_z = Exchange(
                "z", self.box_z, span, None if first else lambda q: self.out.at[rows(q * span, span)]
            )
            self.ex_y = Exchange("y", self.box_y, own, lambda q: self.tot.at[rows(q * own, own)])
            self.ex_x = Exchange("x", self.box_x, own)
            self.ex_r = Exchange("y", self.box_r, own, lambda q: self.ret.at[rows(q * own, own)])

        def hop(self, m):
            return mode(big_s, self.m0 + m)

        def power(self, m, count):
            hop = self.hop(m)
            power, chosen = jnp.ones_like(hop), jnp.ones_like(hop)
            for q in range(1, nz):
                power = power * hop
                chosen = jnp.where(count == q, power, chosen)
            return chosen

        def lower(self, ref_name, start, dynamic=False):
            if self.low is None:
                return None
            ref = getattr(self.low, ref_name)
            return ref[rows(start, ROWS), :] if dynamic else ref[start : start + ROWS, :]

        def begin(self, values):
            if self.first:
                for m in range(HALF):
                    self.box_z[rows(z * span + m * ROWS, ROWS), :] = values[m]
                return
            count = nz - 1 - self.zi
            for m in range(HALF):
                put(self.loc, m, values[m])
                put(self.tot, m, advance(
                    values[m], self.lower("loc", m * ROWS), self.power(m, count), count.astype(F32)))

        def send(self):
            if self.first:
                self.ex_z.start()
            else:
                self.send_y()

        def send_y(self):
            self.ex_y.start()
            self.box_y[mine, :] = self.tot[mine, :]

        def total(self):
            self.ex_z.wait()
            for m in range(HALF):
                hop = self.hop(m)
                running, lower, chosen = zero, zero, zero
                for q in self.order(nz):
                    chosen = jnp.where(z == q, running, chosen)
                    came = mode(self.box_z, m, q * span)
                    if self.low is None:
                        running = hop * running + came
                    else:
                        running = hop * (running + block * lower) + came
                        lower = hop * lower + mode(self.low.box_z, m, q * span)
                put(self.tot, m, running)
                put(self.pre, m, chosen)
            self.send_y()

        def steps(self):
            rho = rho_s[rows((self.m0 + y) * ROWS, ROWS), :]
            return jnp.exp((-nz * block) * rho), jnp.exp((-nz * NY * block) * rho)

        def prefix(self):
            self.ex_y.wait()
            step_y, _ = self.steps()
            running, lower = zero, (None if self.low is None else zero)
            for q in self.order(NY):
                put(self.ret, q, running)
                running = advance(running, lower, step_y, nz) + mode(self.box_y, q)
                if self.low is not None:
                    lower = step_y * lower + mode(self.low.box_y, q)
            self.box_x[rows(x * own, own), :] = running
            self.ex_x.start()

        def give_back(self):
            self.ex_x.wait()
            step_y, step_x = self.steps()
            came, lower = zero, (None if self.low is None else zero)
            for q in self.order(NX):
                earlier = self.before(q)
                came = jnp.where(earlier, advance(came, lower, step_x, nz * NY) + mode(self.box_x, q), came)
                if self.low is not None:
                    lower = jnp.where(earlier, step_x * lower + mode(self.low.box_x, q), lower)
            for q in self.order(NY):
                put(self.ret, q, mode(self.ret, q) + came)
                came = advance(came, lower, step_y, nz)
                if self.low is not None:
                    lower = step_y * lower
            self.ex_r.start()
            self.box_r[mine, :] = self.ret[mine, :]

        def last_z(self):
            self.ex_r.wait()
            for m in range(HALF):
                start, loc = mode(self.box_r, m), mode(self.loc, m)
                start_low, loc_low = self.lower("box_r", m * ROWS), self.lower("loc", m * ROWS)
                hop = self.hop(m)
                power = jnp.ones_like(hop)
                for qi in range(nz):
                    value = advance(start, start_low, power, qi)
                    if qi > 0:
                        count = qi - 1 - self.zi
                        near = advance(loc, loc_low, self.power(m, count), count.astype(F32))
                        value = value + jnp.where(self.zi < qi, near, 0.0)
                    put(self.out, m, value, self.place(qi) * span)
                    power = power * hop
            self.ex_z.start()
            here = rows(z * span, span)
            self.box_z[here, :] = self.out[here, :]

        def arrived(self):
            if self.first:
                self.ex_r.wait()
                return [
                    mode(self.pre, m) + advance(
                        mode(self.box_r, m), self.lower("box_r", m * ROWS),
                        self.power(m, self.zi), self.zi.astype(F32))
                    for m in range(HALF)
                ]
            self.ex_z.wait()
            return [sum(mode(self.box_z, m, q * span) for q in range(1, nz)) + mode(self.box_z, m)
                    for m in range(HALF)]

    sa, sb = Flow("s_first", True, True), Flow("s_last", False, True)
    da, db = Flow("d_first", True, True, sa), Flow("d_last", False, True, sb)
    ga, gb = Flow("g_first", True, False), Flow("g_last", False, False)
    pair = 4 * ROWS
    norms = Exchange("t", box_t, ROWS)
    prm_split = Exchange("y", prm_y, pair, lambda q: prm_s.at[rows(q * pair, pair)])
    prm_sum_x = Exchange("x", prm_x, pair)
    prm_sum_z = Exchange("z", prm_z, pair)
    prm_back = Exchange("y", prm_g, pair)

    loads = [
        pltpu.make_async_copy(src, dst, in_sem.at[i])
        for i, (src, dst) in enumerate([
            (log_rates_hbm, log_rates_v), (residues_hbm, residues_v), (inner_hbm, inner_v),
            (signal_hbm, signal_v), (outer_hbm, outer_v), (cot_hbm, cot_v), (gain_hbm, gain_v),
        ])
    ]
    for load in loads:
        load.start()

    barrier = pltpu.get_barrier_semaphore()
    partners = 0
    for axis in ("z", "y", "x", "t"):
        n, me, device = places[axis]
        for k in range(1, n):
            pl.semaphore_signal(
                barrier, inc=1, device_id=device(lax.rem(me + k, n)), device_id_type=MESH
            )
            partners += 1

    loads[0].wait()
    loads[1].wait()
    for half in range(MODES // 8):
        for j in range(ROWS):
            there = pl.ds(half * 64 + j, 8, stride=ROWS)
            lanes = slice(j * LANES, (j + 1) * LANES)
            rho = jnp.exp(log_rates_v[half * 8 : half * 8 + 8, lanes])
            root = jnp.sqrt(2.0 * rho)
            rho_s[there, :] = rho
            root_s[there, :] = root
            wts_s[there, :] = residues_v[half * 8 : half * 8 + 8, lanes] * root
    lam_s[...] = jnp.exp(-rho_s[...])
    big_s[...] = jnp.exp(-block * rho_s[...])

    def natural(body, step=16):
        def turn(i, carry):
            tokens = rows(i * step, step)
            for j in range(ROWS):
                body(tokens, slice(j * LANES, (j + 1) * LANES),
                     pl.ds(i * (step * ROWS) + j, step, stride=ROWS))
            return carry

        lax.fori_loop(0, length // step, turn, 0)

    def sweep(body, carry, unroll=8, reverse=False):
        def turn(i, carry):
            for u in range(unroll):
                token = i * unroll + u
                if reverse:
                    token = length - 1 - token
                carry = body(rows(token * ROWS, ROWS), carry)
            return carry

        return lax.fori_loop(0, length // unroll, turn, carry)

    def tree(terms):
        while len(terms) > 1:
            terms = [a + b for a, b in zip(terms[::2], terms[1::2])]
        return terms[0]

    loads[2].wait()
    loads[3].wait()

    def multiply(tokens, lanes, place):
        tokens_p[place, :] = inner_v[tokens, lanes].astype(F32) * signal_v[tokens, lanes].astype(F32)

    natural(multiply)

    decay = [mode(lam_s, m) for m in range(MODES)]

    def leave(token, state):
        p = tokens_p[token, :]
        return tuple(d * s + p for d, s in zip(decay, state))

    state = sweep(leave, (zero,) * MODES)
    sa.begin(state[:HALF])
    sb.begin(state[HALF:])
    pl.semaphore_wait(barrier, partners)
    sa.send()
    sb.send()

    for half, flow in enumerate((da, db)):
        some = range(half * HALF, half * HALF + HALF)
        decay8 = [mode(lam_s, m) for m in some]
        weight8 = [mode(wts_s, m) for m in some]

        def respond(token, carry, decay=decay8, weight=weight8, half=half):
            p = tokens_p[token, :]
            lagged = [d * (a + s) for d, a, s in zip(decay, carry[HALF:], carry[:HALF])]
            state = [d * s + p for d, s in zip(decay, carry[:HALF])]
            here = tree([w * s for w, s in zip(weight, state)])
            tokens_r[token, :] = here if half == 0 else tokens_r[token, :] + here
            return tuple(state + lagged)

        flow.begin(sweep(respond, (zero,) * MODES)[HALF:])

    sb.prefix()
    sa.total()
    db.send()
    da.send()
    sb.give_back()
    db.prefix()
    sa.prefix()
    sb.last_z()
    da.total()
    sa.give_back()
    db.give_back()
    da.prefix()

    loads[4].wait()
    loads[5].wait()
    loads[6].wait()
    gain_ref[...] = gain_v[...].astype(F32)[None, :]
    fade = []
    for m, value in enumerate(sa.arrived() + sb.arrived()):
        put(at["state_in"], m, value)
        fade.append(mode(wts_s, m) * value)

    def carried(token, fade):
        fade = tuple(d * f for d, f in zip(decay, fade))
        tokens_r[token, :] = tokens_r[token, :] + tree(list(fade))
        return fade

    sweep(carried, tuple(fade))

    def mix(i, carry):
        tokens = rows(i * 16, 16)
        squares = jnp.zeros((16, LANES), F32)
        inners = jnp.zeros((16, LANES), F32)
        for j in range(ROWS):
            lanes = slice(j * LANES, (j + 1) * LANES)
            mixed = outer_v[tokens, lanes].astype(F32) * tokens_r[pl.ds(i * 128 + j, 16, stride=ROWS), :]
            gained = cot_v[tokens, lanes].astype(F32) * gain_ref[:, lanes]
            mixed_n[tokens, lanes] = mixed
            squares = squares + mixed * mixed
            inners = inners + gained * mixed
        at["sums_a"][tokens, :] = squares
        at["sums_b"][tokens, :] = inners
        return carry

    lax.fori_loop(0, length // 16, mix, 0)

    def across(a, b):
        return lax.dot_general(
            a, b, (((1,), (1,)), ((), ())), precision=lax.Precision.HIGHEST,
            preferred_element_type=F32,
        )

    ones = jnp.ones((ROWS, LANES), F32)
    upper = lax.broadcasted_iota(jnp.int32, (ROWS, length), 0) < 4
    box_t[rows(t * ROWS, ROWS), :] = jnp.where(
        upper, across(ones, at["sums_a"][...]), across(ones, at["sums_b"][...])
    )
    norms.start()
    db.last_z()
    da.give_back()

    norms.wait()
    both = jnp.zeros((ROWS, length), F32)
    for q in range(nt):
        both = both + mode(box_t, q)
    scale = lax.rsqrt(both[0:1, :] / D + 1e-06)
    pull = scale * scale * scale * both[4:5, :] / D
    row_id = lax.broadcasted_iota(jnp.int32, (length, length), 0)
    col_id = lax.broadcasted_iota(jnp.int32, (length, length), 1)
    square = jnp.ones((LANES, length), F32)
    at["cols_a"][...] = across(jnp.where(row_id == col_id, scale, 0.0), square)
    at["cols_b"][...] = across(jnp.where(row_id == col_id, pull, 0.0), square)

    def finish(i, carry):
        tokens = rows(i * 16, 16)
        a, b = at["cols_a"][tokens, :], at["cols_b"][tokens, :]
        for j in range(ROWS):
            lanes = slice(j * LANES, (j + 1) * LANES)
            place = pl.ds(i * 128 + j, 16, stride=ROWS)
            mixed = mixed_n[tokens, lanes]
            gain = gain_ref[:, lanes]
            gained = cot_v[tokens, lanes].astype(F32) * gain
            grad = a * gained - mixed * b
            tokens_w[place, :] = grad * outer_v[tokens, lanes].astype(F32)
            output_ref[tokens, lanes] = (mixed * a * gain).astype(BF16)
            gouter_ref[tokens, lanes] = (grad * tokens_r[place, :]).astype(BF16)
        return carry

    lax.fori_loop(0, length // 16, finish, 0)

    def leave_back(token, adjoint):
        w = tokens_w[token, :]
        return tuple(d * a + w for d, a in zip(decay, adjoint))

    adjoint = sweep(leave_back, (zero,) * MODES, reverse=True)
    adjoint = [d * a for d, a in zip(decay, adjoint)]
    ga.begin(adjoint[:HALF])
    gb.begin(adjoint[HALF:])
    ga.send()
    gb.send()

    for m, value in enumerate(da.arrived() + db.arrived()):
        put(at["stated_in"], m, value)

    for half in range(2):
        some = range(half * HALF, half * HALF + HALF)
        decay8 = [mode(lam_s, m) for m in some]

        def correlate(token, carry, decay=decay8):
            p, w = tokens_p[token, :], tokens_w[token, :]
            state, lagged, first, second = carry[:8], carry[8:16], carry[16:24], carry[24:]
            lagged = [d * (a + s) for d, a, s in zip(decay, lagged, state)]
            state = [d * s + p for d, s in zip(decay, state)]
            first = [f + w * s for f, s in zip(first, state)]
            second = [f + w * a for f, a in zip(second, lagged)]
            return tuple(state + lagged + first + second)

        carry = sweep(
            correlate,
            tuple(mode(at["state_in"], m) for m in some)
            + tuple(mode(at["stated_in"], m) for m in some)
            + (zero,) * 16,
            unroll=4,
        )
        for i, m in enumerate(some):
            base = (m // 2) * pair + (m % 2) * ROWS
            prm_s[base : base + ROWS, :] = carry[16 + i]
            prm_s[base + pair // 2 : base + pair // 2 + ROWS, :] = carry[24 + i]
    prm_split.start()
    prm_y[rows(y * pair, pair), :] = prm_s[rows(y * pair, pair), :]

    def add_up(box, n):
        total = box[0:pair, :]
        for q in range(1, n):
            total = total + box[q * pair : (q + 1) * pair, :]
        return total

    gb.prefix()
    ga.total()

    for half in range(2):
        some = range(half * HALF, half * HALF + HALF)
        decay8 = [mode(lam_s, m) for m in some]
        weight8 = [mode(wts_s, m) for m in some]

        def pull_back(token, adjoint, decay=decay8, weight=weight8, half=half):
            w = tokens_w[token, :]
            adjoint = tuple(d * a + w for d, a in zip(decay, adjoint))
            here = tree([k * a for k, a in zip(weight, adjoint)])
            tokens_r[token, :] = here if half == 0 else tokens_r[token, :] + here
            return adjoint

        sweep(pull_back, (zero,) * HALF, reverse=True)

    gb.give_back()
    prm_split.wait()
    prm_x[rows(x * pair, pair), :] = add_up(prm_y, NY)
    prm_sum_x.start()
    ga.prefix()
    prm_sum_x.wait()
    prm_z[rows(z * pair, pair), :] = add_up(prm_x, NX)
    prm_sum_z.start()
    gb.last_z()
    ga.give_back()
    prm_sum_z.wait()
    prm_g[rows(y * pair, pair), :] = add_up(prm_z, nz)
    prm_back.start()

    fade = tuple(
        mode(wts_s, m) * value for m, value in enumerate(ga.arrived() + gb.arrived())
    )

    def carried_back(token, fade):
        tokens_r[token, :] = tokens_r[token, :] + tree(list(fade))
        return tuple(d * f for d, f in zip(decay, fade))

    sweep(carried_back, fade, reverse=True)

    def last(tokens, lanes, place):
        grad = tokens_r[place, :]
        ginner_ref[tokens, lanes] = (grad * signal_v[tokens, lanes].astype(F32)).astype(BF16)
        gsignal_ref[tokens, lanes] = (grad * inner_v[tokens, lanes].astype(F32)).astype(BF16)

    natural(last)

    prm_back.wait()
    whole = MODES * ROWS
    for m in range(MODES):
        base = (m // 2) * pair + (m % 2) * ROWS
        first = prm_g[base : base + ROWS, :]
        second = prm_g[base + pair // 2 : base + pair // 2 + ROWS, :]
        put(fin_s, m, factor * (mode(root_s, m) * first))
        put(fin_s, m, factor * (mode(wts_s, m) * (0.5 * first - mode(rho_s, m) * second)), whole)
    for half in range(MODES // 8):
        for j in range(ROWS):
            lanes = slice(j * LANES, (j + 1) * LANES)
            some = slice(half * 8, half * 8 + 8)
            rgrad_ref[some, lanes] = fin_s[pl.ds(half * 64 + j, 8, stride=ROWS), :]
            agrad_ref[some, lanes] = fin_s[pl.ds(whole + half * 64 + j, 8, stride=ROWS), :]
    for exchange in everything:
        exchange.drain()


def deliver(*refs):
    sem = refs[12]
    copies = [pltpu.make_async_copy(refs[i], refs[6 + i], sem.at[i]) for i in range(6)]
    for copy in copies:
        copy.start()
    for copy in copies:
        copy.wait()


def solution(mesh):
    nz, nt = mesh.shape["grp"], mesh.shape["tp"]
    blocks = mesh.shape["ctx"] * nz
    assert mesh.shape["ctx"] == NX * NY

    def step(outer_gate, inner_gate, signal, residues, log_rates, norm_gain, cotangent):
        length, channels = outer_gate.shape
        assert channels == ROWS * LANES and length == LANES and residues.shape[0] == MODES
        factor = 1.0 / math.sqrt(length * blocks)
        wide = pltpu.VMEM((length, channels), BF16)
        params = pltpu.VMEM(residues.shape, F32)
        exchanges = 7 * (2 * (NY - 1) + (NX - 1) + (nz - 1)) + (nt - 1)
        scratch = (
            [wide] * 4 + [params] * 2
            + [pltpu.VMEM((channels,), BF16), pltpu.VMEM((1, channels), F32), pltpu.VMEM((length, channels), F32)]
            + [
                pltpu.SemaphoreType.DMA((7,)),
                pltpu.SemaphoreType.DMA((exchanges,)),
                pltpu.SemaphoreType.DMA((exchanges,)),
            ]
            + [pltpu.VMEM((count, LANES), F32) for count in layout(nz, nt, length).values()]
        )
        vmem = pl.BlockSpec(memory_space=pltpu.VMEM)
        hbm = pl.BlockSpec(memory_space=pltpu.HBM)
        shapes = (jax.ShapeDtypeStruct((length, channels), BF16),) * 4 + (
            jax.ShapeDtypeStruct(residues.shape, F32),
        ) * 2

        def body(*refs):
            kernel(nz, nt, length, factor, *refs)

        results = pl.pallas_call(
            body,
            out_shape=shapes,
            in_specs=[hbm] * 7,
            out_specs=(vmem,) * 6,
            scratch_shapes=scratch,
            compiler_params=pltpu.CompilerParams(
                collective_id=0, has_side_effects=True, vmem_limit_bytes=40 * 1024 * 1024
            ),
            name="hyena",
        )(
            *(
                pltpu.with_memory_space_constraint(a, pltpu.HBM)
                for a in (outer_gate, inner_gate, signal, cotangent, residues, log_rates, norm_gain)
            )
        )
        return pl.pallas_call(
            deliver,
            out_shape=shapes,
            in_specs=[pl.BlockSpec(memory_space=pl.ANY)] * 6,
            out_specs=(hbm,) * 6,
            scratch_shapes=[pltpu.SemaphoreType.DMA((6,))],
            compiler_params=pltpu.CompilerParams(vmem_limit_bytes=4 * 1024 * 1024),
            name="deliver",
        )(*results)

    wide, narrow = P(("ctx", "grp"), "tp"), P(None, "tp")
    return jax.shard_map(
        step,
        mesh=mesh,
        in_specs=(wide, wide, wide, narrow, narrow, P("tp"), wide),
        out_specs=(wide,) * 4 + (narrow,) * 2,
        check_vma=False,
    )
```

```python
import math

import jax
import jax.numpy as jnp
from jax import lax
from jax.experimental import pallas as pl
from jax.experimental.pallas import tpu as pltpu
from jax.sharding import PartitionSpec as P

D = 8192
MODES = 16
ROWS = 8
LANES = 128
NX, NY = 4, 8
MESH = pl.DeviceIdType.MESH
F32 = jnp.float32
BF16 = jnp.bfloat16
HALF = MODES // 2
FLOWS = ("s_first", "s_last", "d_first", "d_last", "g_first", "g_last")


def layout(nz, nt, length):
    span, own = HALF * ROWS, ROWS
    shapes = {"tokens_p": length * ROWS, "tokens_r": length * ROWS, "tokens_w": length * ROWS}
    for name in ("sums_a", "sums_b", "cols_a", "cols_b"):
        shapes[name] = length
    for name in ("rho_s", "root_s", "lam_s", "wts_s", "big_s", "state_in"):
        shapes[name] = MODES * ROWS
    for flow in FLOWS:
        shapes |= {
            flow + ".loc": span, flow + ".out": nz * span, flow + ".box_z": nz * span,
            flow + ".tot": span, flow + ".pre": span, flow + ".box_y": NY * own,
            flow + ".box_x": NX * own, flow + ".ret": NY * own, flow + ".box_r": NY * own,
        }
    pair = 2 * ROWS
    for half in ("p0", "p1"):
        shapes |= {
            half + ".sum": NY * pair, half + ".box_y": NY * pair, half + ".box_z": nz * pair,
            half + ".box_x": NX * pair, half + ".all": NY * pair,
        }
    shapes |= {"tokens_g": length * ROWS, "fin_s": 2 * MODES * ROWS, "box_t": nt * ROWS}
    return shapes


def kernel(
    nz, nt, length, factor,
    outer_hbm, inner_hbm, signal_hbm, cot_hbm, residues_hbm, log_rates_hbm, gain_hbm,
    output_ref, gouter_ref, ginner_ref, gsignal_ref, rgrad_ref, agrad_ref,
    outer_v, inner_v, signal_v, cot_v, residues_v, log_rates_v, gain_v, gain_ref, mixed_n,
    in_sem, send_sem, recv_sem, *scratch,
):
    at = dict(zip(layout(nz, nt, length), scratch))
    tokens_p, tokens_r, tokens_w = at["tokens_p"], at["tokens_r"], at["tokens_w"]
    rho_s, root_s, lam_s, wts_s, big_s = (at[k] for k in ("rho_s", "root_s", "lam_s", "wts_s", "big_s"))
    tokens_g = at["tokens_g"]
    box_t, fin_s = at["box_t"], at["fin_s"]

    ctx = lax.axis_index("ctx")
    x, y = ctx // NY, lax.rem(ctx, NY)
    z = lax.axis_index("grp")
    t = lax.axis_index("tp")
    block = float(length)

    def rows(start, size):
        return pl.ds(pl.multiple_of(start, size), size)

    places = {
        "z": (nz, z, lambda q: {"grp": q}),
        "y": (NY, y, lambda q: {"ctx": x * NY + q}),
        "x": (NX, x, lambda q: {"ctx": q * NY + y}),
        "t": (nt, t, lambda q: {"tp": q}),
    }
    used = [0]

    class Exchange:
        def __init__(self, axis, box, size, piece=None):
            self.n, self.me, self.device = places[axis]
            self.box, self.size = box, size
            self.piece = piece or (lambda q: self.slot(self.me))
            self.first = used[0]
            used[0] += self.n - 1
            self.far_first = sorted(range(1, self.n), key=lambda k: -min(k, self.n - k))

        def slot(self, q):
            return self.box.at[rows(q * self.size, self.size)]

        def copy(self, k, landing):
            peer = lax.rem(self.me + k, self.n)
            source = lax.rem(self.me + self.n - k, self.n)
            return pltpu.make_async_remote_copy(
                src_ref=self.piece(peer),
                dst_ref=self.slot(source if landing else self.me),
                send_sem=send_sem.at[self.first + k - 1],
                recv_sem=recv_sem.at[self.first + k - 1],
                device_id=self.device(peer),
                device_id_type=MESH,
            )

        def start(self):
            for k in self.far_first:
                self.copy(k, False).start()

        def wait(self):
            for k in range(1, self.n):
                self.copy(k, True).wait_recv()

        def drain(self):
            for k in range(1, self.n):
                self.copy(k, False).wait_send()

    span, own = HALF * ROWS, ROWS
    mine = rows(y * own, own)
    zero = jnp.zeros((ROWS, LANES), F32)

    def mode(ref, m, base=0):
        return ref[base + m * ROWS : base + (m + 1) * ROWS, :]

    def put(ref, m, value, base=0):
        ref[base + m * ROWS : base + (m + 1) * ROWS, :] = value

    def advance(value, low, power, count):
        return power * value if low is None else power * (value + (block * count) * low)

    class Flow:
        def __init__(self, name, first, forward, low=None):
            self.first, self.low = first, low
            self.m0 = 0 if first else HALF
            for key in ("loc", "out", "box_z", "tot", "pre", "box_y", "box_x", "ret", "box_r"):
                setattr(self, key, at[name + "." + key])
            self.zi = z if forward else nz - 1 - z
            self.order = lambda n: range(n) if forward else range(n - 1, -1, -1)
            self.place = lambda q: q if forward else nz - 1 - q
            self.before = (lambda q: q < x) if forward else (lambda q: q > x)
            self.ex_z = Exchange(
                "z", self.box_z, span, None if first else lambda q: self.out.at[rows(q * span, span)]
            )
            self.ex_y = Exchange("y", self.box_y, own, lambda q: self.tot.at[rows(q * own, own)])
            self.ex_x = Exchange("x", self.box_x, own)
            self.ex_r = Exchange("y", self.box_r, own, lambda q: self.ret.at[rows(q * own, own)])

        def hop(self, m):
            return mode(big_s, self.m0 + m)

        def power(self, m, count):
            hop = self.hop(m)
            power, chosen = jnp.ones_like(hop), jnp.ones_like(hop)
            for q in range(1, nz):
                power = power * hop
                chosen = jnp.where(count == q, power, chosen)
            return chosen

        def lower(self, ref_name, start, dynamic=False):
            if self.low is None:
                return None
            ref = getattr(self.low, ref_name)
            return ref[rows(start, ROWS), :] if dynamic else ref[start : start + ROWS, :]

        def begin(self, values):
            if self.first:
                for m in range(HALF):
                    self.box_z[rows(z * span + m * ROWS, ROWS), :] = values[m]
                return
            count = nz - 1 - self.zi
            for m in range(HALF):
                put(self.loc, m, values[m])
                put(self.tot, m, advance(
                    values[m], self.lower("loc", m * ROWS), self.power(m, count), count.astype(F32)))

        def send(self):
            if self.first:
                self.ex_z.start()
            else:
                self.send_y()

        def send_y(self):
            self.ex_y.start()
            self.box_y[mine, :] = self.tot[mine, :]

        def total(self):
            self.ex_z.wait()
            for m in range(HALF):
                hop = self.hop(m)
                running, lower, chosen = zero, zero, zero
                for q in self.order(nz):
                    chosen = jnp.where(z == q, running, chosen)
                    came = mode(self.box_z, m, q * span)
                    if self.low is None:
                        running = hop * running + came
                    else:
                        running = hop * (running + block * lower) + came
                        lower = hop * lower + mode(self.low.box_z, m, q * span)
                put(self.tot, m, running)
                put(self.pre, m, chosen)
            self.send_y()

        def steps(self):
            rho = rho_s[rows((self.m0 + y) * ROWS, ROWS), :]
            return jnp.exp((-nz * block) * rho), jnp.exp((-nz * NY * block) * rho)

        def prefix(self):
            self.ex_y.wait()
            step_y, _ = self.steps()
            running, lower = zero, (None if self.low is None else zero)
            for q in self.order(NY):
                put(self.ret, q, running)
                running = advance(running, lower, step_y, nz) + mode(self.box_y, q)
                if self.low is not None:
                    lower = step_y * lower + mode(self.low.box_y, q)
            self.box_x[rows(x * own, own), :] = running
            self.ex_x.start()

        def give_back(self):
            self.ex_x.wait()
            step_y, step_x = self.steps()
            came, lower = zero, (None if self.low is None else zero)
            for q in self.order(NX):
                earlier = self.before(q)
                came = jnp.where(earlier, advance(came, lower, step_x, nz * NY) + mode(self.box_x, q), came)
                if self.low is not None:
                    lower = jnp.where(earlier, step_x * lower + mode(self.low.box_x, q), lower)
            for q in self.order(NY):
                put(self.ret, q, mode(self.ret, q) + came)
                came = advance(came, lower, step_y, nz)
                if self.low is not None:
                    lower = step_y * lower
            self.ex_r.start()
            self.box_r[mine, :] = self.ret[mine, :]

        def last_z(self):
            self.ex_r.wait()
            for m in range(HALF):
                start, loc = mode(self.box_r, m), mode(self.loc, m)
                start_low, loc_low = self.lower("box_r", m * ROWS), self.lower("loc", m * ROWS)
                hop = self.hop(m)
                power = jnp.ones_like(hop)
                for qi in range(nz):
                    value = advance(start, start_low, power, qi)
                    if qi > 0:
                        count = qi - 1 - self.zi
                        near = advance(loc, loc_low, self.power(m, count), count.astype(F32))
                        value = value + jnp.where(self.zi < qi, near, 0.0)
                    put(self.out, m, value, self.place(qi) * span)
                    power = power * hop
            self.ex_z.start()
            here = rows(z * span, span)
            self.box_z[here, :] = self.out[here, :]

        def arrived(self):
            if self.first:
                self.ex_r.wait()
                return [
                    mode(self.pre, m) + advance(
                        mode(self.box_r, m), self.lower("box_r", m * ROWS),
                        self.power(m, self.zi), self.zi.astype(F32))
                    for m in range(HALF)
                ]
            self.ex_z.wait()
            return [sum(mode(self.box_z, m, q * span) for q in range(1, nz)) + mode(self.box_z, m)
                    for m in range(HALF)]

    sa, sb = Flow("s_first", True, True), Flow("s_last", False, True)
    da, db = Flow("d_first", True, True, sa), Flow("d_last", False, True, sb)
    ga, gb = Flow("g_first", True, False), Flow("g_last", False, False)
    norms = Exchange("t", box_t, ROWS)
    pair = 2 * ROWS

    class Total:
        def __init__(self, name):
            for key in ("sum", "box_y", "box_z", "box_x", "all"):
                setattr(self, key, at[name + "." + key])
            self.ex_y = Exchange("y", self.box_y, pair, lambda q: self.sum.at[rows(q * pair, pair)])
            self.ex_z = Exchange("z", self.box_z, pair)
            self.ex_x = Exchange("x", self.box_x, pair)
            self.ex_all = Exchange("y", self.all, pair)

        def split(self):
            self.ex_y.start()
            here = rows(y * pair, pair)
            self.box_y[here, :] = self.sum[here, :]

        def hand_on(self, exchange, following):
            exchange.wait()
            total = exchange.box[0:pair, :]
            for q in range(1, exchange.n):
                total = total + exchange.box[q * pair : (q + 1) * pair, :]
            following.box[rows(following.me * pair, pair), :] = total
            following.start()

        def over_z(self):
            self.hand_on(self.ex_y, self.ex_z)

        def over_x(self):
            self.hand_on(self.ex_z, self.ex_x)

        def to_all(self):
            self.hand_on(self.ex_x, self.ex_all)

    totals = (Total("p0"), Total("p1"))

    loads = [
        pltpu.make_async_copy(src, dst, in_sem.at[i])
        for i, (src, dst) in enumerate([
            (log_rates_hbm, log_rates_v), (residues_hbm, residues_v), (inner_hbm, inner_v),
            (signal_hbm, signal_v), (outer_hbm, outer_v), (cot_hbm, cot_v), (gain_hbm, gain_v),
        ])
    ]
    for load in loads:
        load.start()

    barrier = pltpu.get_barrier_semaphore()
    partners = 0
    for axis in ("z", "y", "x", "t"):
        n, me, device = places[axis]
        for k in range(1, n):
            pl.semaphore_signal(
                barrier, inc=1, device_id=device(lax.rem(me + k, n)), device_id_type=MESH
            )
            partners += 1

    loads[0].wait()
    loads[1].wait()
    for half in range(MODES // 8):
        for j in range(ROWS):
            there = pl.ds(half * 64 + j, 8, stride=ROWS)
            lanes = slice(j * LANES, (j + 1) * LANES)
            rho = jnp.exp(log_rates_v[half * 8 : half * 8 + 8, lanes])
            root = jnp.sqrt(2.0 * rho)
            rho_s[there, :] = rho
            root_s[there, :] = root
            wts_s[there, :] = residues_v[half * 8 : half * 8 + 8, lanes] * root
    lam_s[...] = jnp.exp(-rho_s[...])
    big_s[...] = jnp.exp(-block * rho_s[...])

    def natural(body, step=16):
        def turn(i, carry):
            tokens = rows(i * step, step)
            for j in range(ROWS):
                body(tokens, slice(j * LANES, (j + 1) * LANES),
                     pl.ds(i * (step * ROWS) + j, step, stride=ROWS))
            return carry

        lax.fori_loop(0, length // step, turn, 0)

    def sweep(body, carry, unroll=8, reverse=False):
        def turn(i, carry):
            for u in range(unroll):
                token = i * unroll + u
                if reverse:
                    token = length - 1 - token
                carry = body(rows(token * ROWS, ROWS), carry)
            return carry

        return lax.fori_loop(0, length // unroll, turn, carry)

    def tree(terms):
        while len(terms) > 1:
            terms = [a + b for a, b in zip(terms[::2], terms[1::2])]
        return terms[0]

    loads[2].wait()
    loads[3].wait()

    def multiply(tokens, lanes, place):
        tokens_p[place, :] = inner_v[tokens, lanes].astype(F32) * signal_v[tokens, lanes].astype(F32)

    natural(multiply)

    decay = [mode(lam_s, m) for m in range(MODES)]

    def leave(token, state):
        p = tokens_p[token, :]
        return tuple(d * s + p for d, s in zip(decay, state))

    state = sweep(leave, (zero,) * MODES)
    sa.begin(state[:HALF])
    sb.begin(state[HALF:])
    pl.semaphore_wait(barrier, partners)
    sa.send()
    sb.send()

    for half, flow in enumerate((da, db)):
        some = range(half * HALF, half * HALF + HALF)
        decay8 = [mode(lam_s, m) for m in some]
        weight8 = [mode(wts_s, m) for m in some]

        def respond(token, carry, decay=decay8, weight=weight8, half=half):
            p = tokens_p[token, :]
            lagged = [d * (a + s) for d, a, s in zip(decay, carry[HALF:], carry[:HALF])]
            state = [d * s + p for d, s in zip(decay, carry[:HALF])]
            here = tree([w * s for w, s in zip(weight, state)])
            tokens_r[token, :] = here if half == 0 else tokens_r[token, :] + here
            return tuple(state + lagged)

        flow.begin(sweep(respond, (zero,) * MODES)[HALF:])

    sb.prefix()
    sa.total()
    db.send()
    da.send()
    sb.give_back()
    db.prefix()
    sa.prefix()
    sb.last_z()
    da.total()
    sa.give_back()
    db.give_back()
    da.prefix()

    loads[4].wait()
    loads[5].wait()
    loads[6].wait()
    gain_ref[...] = gain_v[...].astype(F32)[None, :]
    fade = []
    for m, value in enumerate(sa.arrived() + sb.arrived()):
        put(at["state_in"], m, value)
        fade.append(mode(wts_s, m) * value)

    def carried(token, fade):
        fade = tuple(d * f for d, f in zip(decay, fade))
        tokens_r[token, :] = tokens_r[token, :] + tree(list(fade))
        return fade

    sweep(carried, tuple(fade))

    def mix(i, carry):
        tokens = rows(i * 16, 16)
        squares = jnp.zeros((16, LANES), F32)
        inners = jnp.zeros((16, LANES), F32)
        for j in range(ROWS):
            lanes = slice(j * LANES, (j + 1) * LANES)
            mixed = outer_v[tokens, lanes].astype(F32) * tokens_r[pl.ds(i * 128 + j, 16, stride=ROWS), :]
            gained = cot_v[tokens, lanes].astype(F32) * gain_ref[:, lanes]
            mixed_n[tokens, lanes] = mixed
            squares = squares + mixed * mixed
            inners = inners + gained * mixed
        at["sums_a"][tokens, :] = squares
        at["sums_b"][tokens, :] = inners
        return carry

    lax.fori_loop(0, length // 16, mix, 0)

    def across(a, b):
        ones_first = a.dtype == BF16
        left, parts = (b if ones_first else a), []
        for _ in range(3):
            parts.append(left.astype(BF16))
            left = left - parts[-1].astype(F32)
        return sum(
            lax.dot_general(
                *((a, part) if ones_first else (part, b)), (((1,), (1,)), ((), ())),
                preferred_element_type=F32,
            )
            for part in reversed(parts)
        )

    ones = jnp.ones((ROWS, LANES), BF16)
    upper = lax.broadcasted_iota(jnp.int32, (ROWS, length), 0) < 4
    box_t[rows(t * ROWS, ROWS), :] = jnp.where(
        upper, across(ones, at["sums_a"][...]), across(ones, at["sums_b"][...])
    )
    norms.start()
    db.last_z()
    da.give_back()

    norms.wait()
    both = jnp.zeros((ROWS, length), F32)
    for q in range(nt):
        both = both + mode(box_t, q)
    scale = lax.rsqrt(both[0:1, :] / D + 1e-06)
    pull = scale * scale * scale * both[4:5, :] / D
    row_id = lax.broadcasted_iota(jnp.int32, (length, length), 0)
    col_id = lax.broadcasted_iota(jnp.int32, (length, length), 1)
    square = jnp.ones((LANES, length), BF16)
    at["cols_a"][...] = across(jnp.where(row_id == col_id, scale, 0.0), square)
    at["cols_b"][...] = across(jnp.where(row_id == col_id, pull, 0.0), square)

    def finish(i, carry):
        tokens = rows(i * 16, 16)
        a, b = at["cols_a"][tokens, :], at["cols_b"][tokens, :]
        for j in range(ROWS):
            lanes = slice(j * LANES, (j + 1) * LANES)
            place = pl.ds(i * 128 + j, 16, stride=ROWS)
            mixed = mixed_n[tokens, lanes]
            gain = gain_ref[:, lanes]
            gained = cot_v[tokens, lanes].astype(F32) * gain
            grad = a * gained - mixed * b
            tokens_w[place, :] = grad * outer_v[tokens, lanes].astype(F32)
        return carry

    lax.fori_loop(0, length // 16, finish, 0)

    def outputs(i, carry):
        tokens = rows(i * 16, 16)
        a, b = at["cols_a"][tokens, :], at["cols_b"][tokens, :]
        for j in range(ROWS):
            lanes = slice(j * LANES, (j + 1) * LANES)
            mixed = mixed_n[tokens, lanes]
            gain = gain_ref[:, lanes]
            gained = cot_v[tokens, lanes].astype(F32) * gain
            grad = a * gained - mixed * b
            response = tokens_r[pl.ds(i * 128 + j, 16, stride=ROWS), :]
            output_ref[tokens, lanes] = (mixed * a * gain).astype(BF16)
            gouter_ref[tokens, lanes] = (grad * response).astype(BF16)
        return carry

    late = [mode(lam_s, m) for m in range(HALF, MODES)]

    def leave_back(token, adjoint):
        w = tokens_w[token, :]
        return tuple(d * a + w for d, a in zip(late, adjoint))

    gb.begin([d * a for d, a in zip(late, sweep(leave_back, (zero,) * HALF, reverse=True))])
    gb.send()

    for half in range(2):
        some = range(half * HALF, half * HALF + HALF)
        decay8 = [mode(lam_s, m) for m in some]

        def correlate(token, carry, decay=decay8):
            p, w = tokens_p[token, :], tokens_w[token, :]
            adjoint, lagged, first, second = carry[:8], carry[8:16], carry[16:24], carry[24:]
            lagged = [d * (b + a) for d, b, a in zip(decay, lagged, adjoint)]
            adjoint = [d * a + w for d, a in zip(decay, adjoint)]
            first = [f + p * a for f, a in zip(first, adjoint)]
            second = [f + p * b for f, b in zip(second, lagged)]
            return tuple(adjoint + lagged + first + second)

        carry = sweep(correlate, (zero,) * 32, unroll=4, reverse=True)
        leaving = [d * a for d, a in zip(decay8, carry[:8])]
        leaving_lagged = [d * (b + a) for d, b, a in zip(decay8, carry[8:16], carry[:8])]
        if half == 0:
            ga.begin(leaving)
            ga.send()
        lagged_in = (da, db)[half].arrived()
        for i, m in enumerate(some):
            start = mode(at["state_in"], m)
            put(totals[half].sum, 2 * i, carry[16 + i] + leaving[i] * start)
            put(totals[half].sum, 2 * i + 1,
                carry[24 + i] + leaving_lagged[i] * start + leaving[i] * lagged_in[i])
        totals[half].split()

    gb.prefix()
    totals[0].over_z()
    gb.give_back()
    ga.total()
    totals[1].over_z()

    for half in range(2):
        some = range(half * HALF, half * HALF + HALF)
        decay8 = [mode(lam_s, m) for m in some]
        weight8 = [mode(wts_s, m) for m in some]

        def pull_back(token, adjoint, decay=decay8, weight=weight8, half=half):
            w = tokens_w[token, :]
            adjoint = tuple(d * a + w for d, a in zip(decay, adjoint))
            here = tree([k * a for k, a in zip(weight, adjoint)])
            tokens_g[token, :] = here if half == 0 else tokens_g[token, :] + here
            return adjoint

        sweep(pull_back, (zero,) * HALF, reverse=True)

    totals[0].over_x()
    gb.last_z()
    ga.prefix()
    totals[1].over_x()
    totals[0].to_all()
    ga.give_back()
    lax.fori_loop(0, length // 16, outputs, 0)
    totals[1].to_all()
    for flow in (sa, sb, da, db):
        for exchange in (flow.ex_z, flow.ex_y, flow.ex_x, flow.ex_r):
            exchange.drain()
    norms.drain()

    fade = tuple(
        mode(wts_s, m) * value for m, value in enumerate(ga.arrived() + gb.arrived())
    )

    def carried_back(token, fade):
        tokens_g[token, :] = tokens_g[token, :] + tree(list(fade))
        return tuple(d * f for d, f in zip(decay, fade))

    sweep(carried_back, fade, reverse=True)

    def last(tokens, lanes, place):
        grad = tokens_g[place, :]
        ginner_ref[tokens, lanes] = (grad * signal_v[tokens, lanes].astype(F32)).astype(BF16)
        gsignal_ref[tokens, lanes] = (grad * inner_v[tokens, lanes].astype(F32)).astype(BF16)

    natural(last)

    whole = MODES * ROWS
    for m in range(MODES):
        if m % HALF == 0:
            totals[m // HALF].ex_all.wait()
        first = mode(totals[m // HALF].all, 2 * (m % HALF))
        second = mode(totals[m // HALF].all, 2 * (m % HALF) + 1)
        put(fin_s, m, factor * (mode(root_s, m) * first))
        put(fin_s, m, factor * (mode(wts_s, m) * (0.5 * first - mode(rho_s, m) * second)), whole)
    for half in range(MODES // 8):
        for j in range(ROWS):
            lanes = slice(j * LANES, (j + 1) * LANES)
            some = slice(half * 8, half * 8 + 8)
            rgrad_ref[some, lanes] = fin_s[pl.ds(half * 64 + j, 8, stride=ROWS), :]
            agrad_ref[some, lanes] = fin_s[pl.ds(whole + half * 64 + j, 8, stride=ROWS), :]
    for flow in (ga, gb):
        for exchange in (flow.ex_z, flow.ex_y, flow.ex_x, flow.ex_r):
            exchange.drain()
    for total in totals:
        for exchange in (total.ex_y, total.ex_z, total.ex_x, total.ex_all):
            exchange.drain()


def deliver(*refs):
    sem = refs[12]
    copies = [pltpu.make_async_copy(refs[i], refs[6 + i], sem.at[i]) for i in range(6)]
    for copy in copies:
        copy.start()
    for copy in copies:
        copy.wait()


def solution(mesh):
    nz, nt = mesh.shape["grp"], mesh.shape["tp"]
    blocks = mesh.shape["ctx"] * nz
    assert mesh.shape["ctx"] == NX * NY

    def step(outer_gate, inner_gate, signal, residues, log_rates, norm_gain, cotangent):
        length, channels = outer_gate.shape
        assert channels == ROWS * LANES and length == LANES and residues.shape[0] == MODES
        factor = 1.0 / math.sqrt(length * blocks)
        wide = pltpu.VMEM((length, channels), BF16)
        params = pltpu.VMEM(residues.shape, F32)
        exchanges = 8 * (2 * (NY - 1) + (NX - 1) + (nz - 1)) + (nt - 1)
        scratch = (
            [wide] * 4 + [params] * 2
            + [pltpu.VMEM((channels,), BF16), pltpu.VMEM((1, channels), F32), pltpu.VMEM((length, channels), F32)]
            + [
                pltpu.SemaphoreType.DMA((7,)),
                pltpu.SemaphoreType.DMA((exchanges,)),
                pltpu.SemaphoreType.DMA((exchanges,)),
            ]
            + [pltpu.VMEM((count, LANES), F32) for count in layout(nz, nt, length).values()]
        )
        vmem = pl.BlockSpec(memory_space=pltpu.VMEM)
        hbm = pl.BlockSpec(memory_space=pltpu.HBM)
        shapes = (jax.ShapeDtypeStruct((length, channels), BF16),) * 4 + (
            jax.ShapeDtypeStruct(residues.shape, F32),
        ) * 2

        def body(*refs):
            kernel(nz, nt, length, factor, *refs)

        results = pl.pallas_call(
            body,
            out_shape=shapes,
            in_specs=[hbm] * 7,
            out_specs=(vmem,) * 6,
            scratch_shapes=scratch,
            compiler_params=pltpu.CompilerParams(
                collective_id=0, has_side_effects=True, vmem_limit_bytes=40 * 1024 * 1024
            ),
            name="hyena",
        )(
            *(
                pltpu.with_memory_space_constraint(a, pltpu.HBM)
                for a in (outer_gate, inner_gate, signal, cotangent, residues, log_rates, norm_gain)
            )
        )
        return pl.pallas_call(
            deliver,
            out_shape=shapes,
            in_specs=[pl.BlockSpec(memory_space=pl.ANY)] * 6,
            out_specs=(hbm,) * 6,
            scratch_shapes=[pltpu.SemaphoreType.DMA((6,))],
            compiler_params=pltpu.CompilerParams(vmem_limit_bytes=4 * 1024 * 1024),
            name="deliver",
        )(*results)

    wide, narrow = P(("ctx", "grp"), "tp"), P(None, "tp")
    return jax.shard_map(
        step,
        mesh=mesh,
        in_specs=(wide, wide, wide, narrow, narrow, P("tp"), wide),
        out_specs=(wide,) * 4 + (narrow,) * 2,
        check_vma=False,
    )
```
